256 devices in a mesh: ctx: 16 (over x, z_lo), sec: 8 (over y, core), dp: 2 (over z_hi).
Axes of the slice: x: 4, y: 4, z: 8 (z_hi: 2, z_lo: 4; z = z_hi * 4 + z_lo), core: 2. Of those that a mesh axis runs over, the one named last changes fastest.
Arguments:
- fresh_input: bfloat16 [2, 4096, 1536], P('dp', 'ctx'), may hold values from -6 to 6
- carried: bfloat16 [8, 2, 4096, 1536], P('sec', 'dp', 'ctx'), may hold values from -6 to 6
- qkv_weight: bfloat16 [8, 1536, 4608], P('sec', ('ctx', 'dp')), as said below
- out_weight: bfloat16 [8, 1536, 1536], P('sec', ('ctx', 'dp')), may hold values from -0.15625 to 0.15625
- rate_weight: bfloat16 [8, 1536, 6], P('sec', ('ctx', 'dp')), may hold values from -0.15625 to 0.15625
- fast_state: float32 [8, 2, 3, 6, 768, 256], P('sec', 'dp', None, None, 'ctx'), may hold values from -6 to 6
Outputs:
- passed: bfloat16 [8, 2, 4096, 1536], P('sec', 'dp', 'ctx')
- new_state: float32 [8, 2, 3, 6, 768, 256], P('sec', 'dp', None, None, 'ctx')
The draws below stay inside these ranges and needn't reach their ends.
Inputs may be any that keep to these rules, and one draw needn't show every extreme that they name: Every entry of qkv_weight is at most 6 / sqrt(1536) in magnitude.
All inputs are finite; a program needn't handle non-finite values.
Results may differ from the reference program's by a relative error of at most 0.022.
Values may be sent and summed in bfloat16 or wider, within the bound.
No kernel may reach another device: no remote copies, remote signals or barrier semaphores. Data moves between devices by JAX's collectives and lax.ppermute only.
A program may use at most 128 MiB of HBM per device.

```python
import jax
import jax.numpy as jnp
from jax import lax

D = 1536
HEADS = 6
HD = 256
FH = 768
NS_STEPS = 2
GROUP = 4096
N_CTX = 16
N_SEC = 8
N_DP = 2


def draw_qkv_weight(key, part):
    columns = 3 * HEADS * HD
    entry_key, pick_key, high_key, low_key = jax.random.split(key, 4)
    entries = jax.random.truncated_normal(entry_key, -6.0, 6.0, (N_SEC, D, columns), jnp.float32)
    high_share = 0.45
    low_bottom = -1.6
    low_top = -1.1
    picked = jax.random.bernoulli(pick_key, high_share, (N_SEC, 1, columns))
    high_scale = jnp.exp(jax.random.uniform(high_key, (N_SEC, 1, columns), jnp.float32, -0.2, 0.0))
    low_scale = jnp.exp(jax.random.uniform(low_key, (N_SEC, 1, columns), jnp.float32, low_bottom, low_top))
    position = jnp.arange(columns, dtype=jnp.int32)[None, None, :]
    column_scale = jnp.where(position >= HEADS * HD, jnp.where(picked, high_scale, low_scale), 1.0)
    return (entries * column_scale * float(D) ** (-0.5)).astype(jnp.bfloat16)


def levels(rng, shape, pieces, least, top_value):
    factor_of = 1.0
    for dim, blocks in pieces:
        heights = jax.random.uniform(jax.random.fold_in(jax.random.fold_in(rng, 6), dim), (blocks,), jnp.float32, least / len(pieces), top_value / len(pieces))
        factor_of = factor_of * jnp.repeat(jnp.exp(heights), shape[dim] // blocks).reshape((-1,) + (1,) * (len(shape) - 1 - dim))
    return factor_of


def centred(own_key, dims, scale, limit, pieces=(), kind=jnp.bfloat16):
    values = jax.random.normal(own_key, dims, jnp.float32) * scale
    if len(pieces) > 0:
        values = levels(own_key, dims, pieces, -0.22, 0.18) * values
    return jnp.clip(values, min=-limit, max=limit).astype(kind)


def setup_inputs(seed: int = 0) -> dict:
    keys = jax.random.split(jax.random.key(seed), 7)
    return {
        "fresh_input": centred(keys[0], (N_DP, GROUP, D), 1.0, 6.0, ((0, 2), (1, 16))),
        "carried": centred(keys[1], (N_SEC, N_DP, GROUP, D), 1.0, 6.0, ((0, 8), (1, 2), (2, 16))),
        "qkv_weight": draw_qkv_weight(jax.random.fold_in(keys[6], 71), 0),
        "out_weight": centred(keys[3], (N_SEC, HEADS * HD, D), (HEADS * HD) ** -0.5, 0.15625, ((0, 8), (1, 32))),
        "rate_weight": centred(keys[4], (N_SEC, D, HEADS), D ** -0.5, 0.15625, ((0, 8), (1, 32))),
        "fast_state": centred(keys[5], (N_SEC, N_DP, 3, HEADS, FH, HD), 1.0, 6.0, ((0, 8), (1, 2), (4, 16)), jnp.float32),
    }


linear_coef = 3.4445
cubic_coef = -4.775
quintic_coef = 2.0315
update_scale = 8.0
highest = lax.Precision.HIGHEST

def swish(values):
    return values * jax.nn.sigmoid(values)

def unit_rows(values):
    return values / jnp.sqrt(lax.optimization_barrier(jnp.sum(values * values, axis=-1, keepdims=True)) + 1e-06)

def to_half(values):
    return lax.optimization_barrier(values.astype(jnp.bfloat16)).astype(jnp.float32)

def group_terms(key_rows, value_rows, rates, gate_fast, up_fast, down_fast):
    keys_wide = key_rows.astype(jnp.float32)
    gate_pre = jnp.einsum('thd,hfd->thf', keys_wide, gate_fast)
    up_pre = jnp.einsum('thd,hfd->thf', keys_wide, up_fast)
    sigma = jax.nn.sigmoid(gate_pre)
    gate_act = gate_pre * sigma
    key_hidden = to_half(gate_act * up_pre)
    scaled_values = to_half(rates[:, :, None] * value_rows.astype(jnp.float32))
    hidden_grad = -jnp.einsum('thd,hfd->thf', scaled_values, down_fast)
    up_grad = to_half(hidden_grad * gate_act)
    gate_grad = to_half(hidden_grad * up_pre * sigma * (1.0 + gate_pre * (1.0 - sigma)))
    grad_gate = jnp.einsum('thf,thd->hfd', gate_grad, keys_wide)
    grad_up = jnp.einsum('thf,thd->hfd', up_grad, keys_wide)
    grad_down = -jnp.einsum('thf,thd->hfd', key_hidden, scaled_values)
    return jnp.stack([grad_gate, grad_up, grad_down])

def gram_sum(current):
    blocks = current.reshape(3, HEADS, N_CTX, FH // N_CTX, HD)
    parts = jnp.einsum('mhnrd,mhnre->mhnde', blocks, blocks, precision=highest)
    return lax.optimization_barrier(jnp.sum(to_half(parts), axis=2))

def orthogonalize(gradient):
    current = gradient
    for iteration in range(NS_STEPS):
        square = gram_sum(current)
        if iteration == 0:
            inverse_norm = lax.rsqrt(jnp.trace(square, axis1=-2, axis2=-1) + 1e-06)[:, :, None, None]
            current = current * inverse_norm
            square = square * inverse_norm * inverse_norm
        product = jnp.einsum('mhrd,mhde->mhre', current, square, precision=highest)
        current = linear_coef * current + cubic_coef * product + quintic_coef * jnp.einsum('mhrd,mhde->mhre', product, square, precision=highest)
    return current

def fast_layer(inputs, qkv_weight, out_weight, rate_weight, fast_state):
    count = inputs.shape[0]
    projected = jnp.dot(inputs, qkv_weight, preferred_element_type=jnp.float32).reshape(count, 3, HEADS, HD)
    query_rows = unit_rows(swish(projected[:, 0])).astype(jnp.bfloat16)
    key_rows = unit_rows(swish(projected[:, 1])).astype(jnp.bfloat16)
    value_rows = projected[:, 2].astype(jnp.bfloat16)
    rates = jax.nn.softplus(jnp.dot(inputs, rate_weight, preferred_element_type=jnp.float32))
    fast_round = to_half(fast_state)
    gate_fast, up_fast, down_fast = (fast_round[0], fast_round[1], fast_round[2])
    query_wide = query_rows.astype(jnp.float32)
    gate_pre = jnp.einsum('thd,hfd->thf', query_wide, gate_fast)
    up_pre = jnp.einsum('thd,hfd->thf', query_wide, up_fast)
    hidden = to_half(swish(gate_pre) * up_pre)
    mixture = jnp.einsum('thf,hfd->thd', hidden, down_fast)
    head_out = (mixture * lax.rsqrt(lax.optimization_barrier(jnp.mean(mixture * mixture, axis=-1, keepdims=True)) + 1e-05)).astype(jnp.bfloat16)
    head_out = head_out.reshape(count, HEADS * HD)
    passed = (inputs.astype(jnp.float32) + jnp.dot(head_out, out_weight, preferred_element_type=jnp.float32)).astype(jnp.bfloat16)

    def add_block(running, block):
        keys_block, values_block, rates_block = block
        term = group_terms(keys_block, values_block, rates_block, gate_fast, up_fast, down_fast)
        return (running + to_half(term), None)
    blocks = (key_rows.reshape(N_CTX, -1, HEADS, HD), value_rows.reshape(N_CTX, -1, HEADS, HD), rates.reshape(N_CTX, -1, HEADS))
    gradient, _ = lax.scan(add_block, jnp.zeros((3, HEADS, FH, HD), jnp.float32), blocks)
    current = orthogonalize(gradient)
    stepped = fast_state - update_scale * current
    rescale = jnp.sqrt(lax.optimization_barrier(jnp.mean(fast_state * fast_state, axis=-1, keepdims=True)) + 1e-06) * lax.rsqrt(lax.optimization_barrier(jnp.mean(stepped * stepped, axis=-1, keepdims=True)) + 1e-06)
    return (passed, stepped * rescale)

def reference(fresh_input, carried, qkv_weight, out_weight, rate_weight, fast_state):
    passed_rows = []
    state_rows = []
    for section in range(N_SEC):
        for sequence in range(N_DP):
            if section == 0:
                inputs = fresh_input[sequence]
            else:
                inputs = carried[section - 1, sequence]
            passed, updated = fast_layer(inputs, qkv_weight[section], out_weight[section], rate_weight[section], fast_state[section, sequence])
            passed_rows.append(passed)
            state_rows.append(updated)
    passed_all = jnp.stack(passed_rows).reshape(N_SEC, N_DP, GROUP, D)
    state_all = jnp.stack(state_rows).reshape(N_SEC, N_DP, 3, HEADS, FH, HD)
    return (passed_all, state_all)
```

```python
import jax
import jax.numpy as jnp
from jax import lax
from jax.sharding import Mesh
from jax.sharding import PartitionSpec as P

CTX = ("xh", "xl", "zl")
CTX_DP = CTX + ("dp",)
LANES = 128

linear_coef = 3.4445
cubic_coef = -4.775
quintic_coef = 2.0315
update_scale = 8.0
highest = lax.Precision.HIGHEST


def swish(values):
    return values * jax.nn.sigmoid(values)


def unit_rows(values):
    return values / jnp.sqrt(jnp.sum(values * values, axis=-1, keepdims=True) + 1e-06)


def swap_pair(block):
    return lax.ppermute(block, "xh", [(0, 1), (1, 0)])


def pair_shard(low, high, is_low, dim):
    kept = jnp.where(is_low, low, high)
    got = swap_pair(jnp.where(is_low, high, low))
    return jnp.concatenate([jnp.where(is_low, kept, got), jnp.where(is_low, got, kept)], axis=dim)


def polynomial(square):
    return (
        linear_coef * jnp.eye(square.shape[-1], dtype=jnp.float32)
        + cubic_coef * square
        + quintic_coef * jnp.einsum("mde,mef->mdf", square, square, precision=highest)
    )


def orthogonalize(gradient):
    square = jnp.einsum("mrd,mre->mde", gradient, gradient, precision=highest)
    inverse_norm = lax.rsqrt(jnp.trace(square, axis1=-2, axis2=-1) + 1e-06)[:, None, None]
    square = square * inverse_norm * inverse_norm
    first = polynomial(square)
    square = jnp.einsum(
        "mde,mef->mdf",
        first,
        jnp.einsum("mde,mef->mdf", square, first, precision=highest),
        precision=highest,
    )
    both = jnp.einsum("mde,mef->mdf", first, polynomial(square), precision=highest)
    return jnp.einsum("mrd,mde->mre", gradient * inverse_norm, both, precision=highest)


def local(fresh_input, carried, qkv_weight, out_weight, rate_weight, fast_state):
    is_low = lax.axis_index("xh") == 0
    sections = lax.axis_size("sec")
    heads = rate_weight.shape[2]
    head_dim = fast_state.shape[5]
    half = heads // 2
    width = half * head_dim
    rows = qkv_weight.shape[1]
    count, channels = fresh_input.shape[1:]

    w = qkv_weight[0].reshape(rows, 3, 2, width)
    rates = jnp.pad(rate_weight[0].reshape(rows, 2, half), ((0, 0), (0, 0), (0, LANES - half)))
    low, high = (
        jnp.concatenate([w[:, 0, h], w[:, 1, h], w[:, 2, h], rates[:, h]], axis=1) for h in (0, 1)
    )
    group_w = lax.all_gather(
        pair_shard(low, high, is_low, 0), ("xl", "zl", "dp"), axis=0, tiled=True
    )
    previous = fast_state[0, 0]
    shard = previous.astype(jnp.bfloat16)
    group_fast = lax.all_gather(
        pair_shard(shard[:, :half], shard[:, half:], is_low, 2), ("xl", "zl"), axis=2, tiled=True
    )
    group_out = lax.all_gather(out_weight[0], ("xl", "zl", "dp"), axis=0, tiled=True)

    is_last = lax.axis_index("sec") == sections - 1
    source = jnp.where(is_last, fresh_input[0], carried[0, 0])
    mine = lax.ppermute(source, "sec", [(i, (i + 1) % sections) for i in range(sections)])
    pairs = [
        (a * sections + i, (1 - a) * sections + (i + 1) % sections)
        for a in (0, 1)
        for i in range(sections)
    ]
    other = lax.ppermute(source, ("xh", "sec"), pairs)
    inputs = jnp.concatenate([mine, other], axis=0)
    ordered = (
        inputs.reshape(2 * count, 2, -1, rows).transpose(0, 2, 1, 3).reshape(2 * count, channels)
    )

    projected = jnp.dot(ordered, group_w, preferred_element_type=jnp.float32)
    part = lambda i: projected[:, i * width : (i + 1) * width].reshape(2 * count, half, head_dim)
    query_rows = unit_rows(swish(part(0))).astype(jnp.bfloat16)
    key_rows = unit_rows(swish(part(1))).astype(jnp.bfloat16)
    value_rows = part(2).astype(jnp.bfloat16)
    rates = jax.nn.softplus(projected[:, 3 * width : 3 * width + half])
    gate_fast, up_fast, down_fast = (group_fast[0], group_fast[1], group_fast[2])

    gate_pre = jnp.einsum("thd,hfd->htf", key_rows, gate_fast, preferred_element_type=jnp.float32)
    up_pre = jnp.einsum("thd,hfd->htf", key_rows, up_fast, preferred_element_type=jnp.float32)
    sigma = jax.nn.sigmoid(gate_pre)
    gate_act = gate_pre * sigma
    key_hidden = (gate_act * up_pre).astype(jnp.bfloat16)
    scaled_values = (rates[:, :, None] * value_rows.astype(jnp.float32)).astype(jnp.bfloat16)
    hidden_grad = -jnp.einsum(
        "thd,hfd->htf", scaled_values, down_fast, preferred_element_type=jnp.float32
    )
    up_grad = (hidden_grad * gate_act).astype(jnp.bfloat16)
    gate_grad = (hidden_grad * up_pre * sigma * (1.0 + gate_pre * (1.0 - sigma))).astype(
        jnp.bfloat16
    )
    grad_gate = jnp.einsum("htf,thd->hfd", gate_grad, key_rows, preferred_element_type=jnp.float32)
    grad_up = jnp.einsum("htf,thd->hfd", up_grad, key_rows, preferred_element_type=jnp.float32)
    grad_down = -jnp.einsum(
        "htf,thd->hfd", key_hidden, scaled_values, preferred_element_type=jnp.float32
    )

    owners = lax.axis_size(("xl", "zl"))
    spread = jnp.concatenate([grad_gate, grad_up, grad_down[: owners - 2 * half]], axis=0)
    shared = lax.psum(grad_down[owners - 2 * half :].astype(jnp.bfloat16), ("xl", "zl"))
    owned = lax.psum_scatter(
        spread.astype(jnp.bfloat16), ("xl", "zl"), scatter_dimension=0, tiled=True
    )
    gradient = jnp.concatenate([owned, shared], axis=0).astype(jnp.float32)
    current = orthogonalize(gradient).astype(jnp.bfloat16)
    shard_rows = previous.shape[2]
    blocks = current.reshape(2, owners, 2, shard_rows, head_dim)
    outgoing = blocks[0].transpose(1, 0, 2, 3).reshape(2 * owners, shard_rows, head_dim)
    arrived = lax.all_to_all(outgoing, CTX, 0, 0, tiled=True)
    arrived = arrived.reshape(2, owners, shard_rows, head_dim)
    mine_last = lax.dynamic_index_in_dim(
        blocks[1], lax.axis_index(("xl", "zl")), 0, keepdims=False
    )
    last = pair_shard(mine_last[0][None], mine_last[1][None], is_low, 0)[:, None]
    current = jnp.concatenate([arrived, last], axis=1).astype(jnp.float32)
    current = current.reshape(2, 3, half, shard_rows, head_dim).transpose(1, 0, 2, 3, 4)
    current = current.reshape(previous.shape)
    stepped = previous - update_scale * current
    rescale = jnp.sqrt(jnp.mean(previous * previous, axis=-1, keepdims=True) + 1e-06) * lax.rsqrt(
        jnp.mean(stepped * stepped, axis=-1, keepdims=True) + 1e-06
    )
    new_state = (stepped * rescale)[None, None]

    gate_query = jnp.einsum(
        "thd,hfd->htf", query_rows, gate_fast, preferred_element_type=jnp.float32
    )
    up_query = jnp.einsum("thd,hfd->htf", query_rows, up_fast, preferred_element_type=jnp.float32)
    hidden = (swish(gate_query) * up_query).astype(jnp.bfloat16)
    mixture = jnp.einsum("htf,hfd->thd", hidden, down_fast, preferred_element_type=jnp.float32)
    head_out = (
        mixture * lax.rsqrt(jnp.mean(mixture * mixture, axis=-1, keepdims=True) + 1e-05)
    ).astype(jnp.bfloat16)
    branch_out = jnp.dot(
        head_out.reshape(2 * count, width), group_out, preferred_element_type=jnp.float32
    )
    from_pair = swap_pair(branch_out[count:].astype(jnp.bfloat16))
    passed = (
        mine.astype(jnp.float32) + (branch_out[:count] + from_pair.astype(jnp.float32))
    ).astype(jnp.bfloat16)
    return (passed[None, None], new_state)


def solution(mesh):
    shape = (2, 2, 4, mesh.shape["sec"], mesh.shape["dp"])
    split = Mesh(mesh.devices.reshape(shape), ("xh", "xl", "zl", "sec", "dp"))
    in_specs = (
        P("dp", CTX, None),
        P("sec", "dp", CTX, None),
        P("sec", CTX_DP, None),
        P("sec", CTX_DP, None),
        P("sec", CTX_DP, None),
        P("sec", "dp", None, None, CTX, None),
    )
    out_specs = (P("sec", "dp", CTX, None), P("sec", "dp", None, None, CTX, None))
    return jax.shard_map(local, mesh=split, in_specs=in_specs, out_specs=out_specs, check_vma=False)
```

```python
import jax
import jax.numpy as jnp
from jax import lax
from jax.sharding import Mesh
from jax.sharding import PartitionSpec as P

CTX = ("xh", "xl", "zl")
CTX_DP = CTX + ("dp",)
SEC = ("y", "c")
LANES = 128

linear_coef = 3.4445
cubic_coef = -4.775
quintic_coef = 2.0315
update_scale = 8.0
highest = lax.Precision.HIGHEST


def swish(values):
    return values * jax.nn.sigmoid(values)


def unit_rows(values):
    return values / jnp.sqrt(jnp.sum(values * values, axis=-1, keepdims=True) + 1e-06)


def swap_axis(block, axis):
    return lax.ppermute(block, axis, [(0, 1), (1, 0)])


def exchange(block, across):
    route = [
        (4 * x + 2 * a + b, 4 * (x ^ across) + 2 * b + a)
        for x in (0, 1)
        for a in (0, 1)
        for b in (0, 1)
    ]
    return lax.ppermute(block, ("xh", "xl", "c"), route)


def from_section_behind(block, across):
    ys = lax.axis_size("y")
    at = lambda x, a, y, b: ((2 * x + a) * ys + y) * 2 + b
    route = []
    for x in (0, 1):
        for layer in (0, 1):
            for y in range(ys):
                for k in (0, 1):
                    behind = (2 * y + layer - 1) % (2 * ys)
                    source = at(x ^ across, k, behind // 2, behind % 2)
                    route.append((source, at(x, layer, y, k)))
    return lax.ppermute(block, ("xh", "xl", "y", "c"), route)


def pair_shard(low, high, is_low, dim):
    kept = exchange(jnp.where(is_low, low, high), 0)
    got = exchange(jnp.where(is_low, high, low), 1)
    return jnp.concatenate([jnp.where(is_low, kept, got), jnp.where(is_low, got, kept)], axis=dim)


def polynomial(square):
    return (
        linear_coef * jnp.eye(square.shape[-1], dtype=jnp.float32)
        + cubic_coef * square
        + quintic_coef * jnp.dot(square, square, precision=highest)
    )


def orthogonalize(gradient, rows):
    square = jnp.einsum("rd,re->de", gradient, gradient, precision=highest)
    inverse_norm = lax.rsqrt(jnp.trace(square) + 1e-06)
    square = square * inverse_norm * inverse_norm
    first = polynomial(square)
    square = jnp.dot(first, jnp.dot(square, first, precision=highest), precision=highest)
    both = jnp.dot(first, polynomial(square), precision=highest)
    return jnp.dot(rows * inverse_norm, both, precision=highest).astype(jnp.bfloat16)


def local(fresh_input, carried, qkv_weight, out_weight, rate_weight, fast_state):
    is_low = lax.axis_index("xh") == 0
    core = lax.axis_index("c")
    is_first = core == 0
    heads = rate_weight.shape[2]
    head_dim = fast_state.shape[5]
    half = heads // 2
    width = half * head_dim
    rows = qkv_weight.shape[1]
    count, channels = fresh_input.shape[1:]
    dots = lambda a, b: jnp.dot(a, b, preferred_element_type=jnp.float32)

    w = qkv_weight[0]
    part = lambda i, h: w[:, (2 * i + h) * width : (2 * i + h + 1) * width]
    rate = lambda h: jnp.pad(
        rate_weight[0][:, h * half : (h + 1) * half], ((0, 0), (0, LANES - half))
    )
    low, high = (jnp.concatenate([part(1, h), part(2, h), rate(h)], axis=1) for h in (0, 1))
    ring = ("dp", "zl")
    my_kv = lax.all_gather(pair_shard(low, high, is_low, 0), ring, axis=0, tiled=True)

    previous = fast_state[0, 0]
    shard = previous.astype(jnp.bfloat16)
    my_fast = lax.all_gather(
        pair_shard(shard[:, :half], shard[:, half:], is_low, 2), "zl", axis=2, tiled=True
    )

    is_last = lax.axis_index(SEC) == lax.axis_size(SEC) - 1
    source = jnp.where(is_last, fresh_input[0], carried[0, 0])
    mine = from_section_behind(source, 0)
    other = from_section_behind(source, 1)
    inputs = jnp.concatenate([mine, other], axis=0)

    my_q = lax.all_gather(
        pair_shard(part(0, 0), part(0, 1), is_low, 0), ring, axis=0, tiled=True
    )
    my_out = lax.all_gather(exchange(out_weight[0], 0), ring, axis=0, tiled=True)

    zs = lax.axis_size("zl")
    ordered = inputs.reshape(2 * count, 2, 2, zs, -1, rows).transpose(2, 0, 4, 3, 1, 5)
    ordered = ordered.reshape(2, 2 * count, channels // 2)
    my_columns = jnp.where(is_first, ordered[0], ordered[1])
    its_columns = jnp.where(is_first, ordered[1], ordered[0])

    its_kv = swap_axis(my_kv, "c")
    projected = dots(my_columns, my_kv) + dots(its_columns, its_kv)
    by_head = lambda a: a.reshape(2 * count, half, head_dim)
    key_rows = unit_rows(swish(by_head(projected[:, :width]))).astype(jnp.bfloat16)
    value_rows = by_head(projected[:, width : 2 * width]).astype(jnp.bfloat16)
    rates = jax.nn.softplus(projected[:, 2 * width : 2 * width + half])

    its_fast = swap_axis(my_fast, "c")
    fast = jnp.concatenate(
        [jnp.where(is_first, my_fast, its_fast), jnp.where(is_first, its_fast, my_fast)], axis=2
    )
    gate_fast, up_fast, down_fast = (fast[0], fast[1], fast[2])

    gate_pre = jnp.einsum("thd,hfd->htf", key_rows, gate_fast, preferred_element_type=jnp.float32)
    up_pre = jnp.einsum("thd,hfd->htf", key_rows, up_fast, preferred_element_type=jnp.float32)
    sigma = jax.nn.sigmoid(gate_pre)
    gate_act = gate_pre * sigma
    key_hidden = (gate_act * up_pre).astype(jnp.bfloat16)
    scaled_values = (rates[:, :, None] * value_rows.astype(jnp.float32)).astype(jnp.bfloat16)
    hidden_grad = -jnp.einsum(
        "thd,hfd->htf", scaled_values, down_fast, preferred_element_type=jnp.float32
    )
    up_grad = (hidden_grad * gate_act).astype(jnp.bfloat16)
    gate_grad = (hidden_grad * up_pre * sigma * (1.0 + gate_pre * (1.0 - sigma))).astype(
        jnp.bfloat16
    )
    grad_gate = jnp.einsum("htf,thd->hfd", gate_grad, key_rows, preferred_element_type=jnp.float32)
    grad_up = jnp.einsum("htf,thd->hfd", up_grad, key_rows, preferred_element_type=jnp.float32)
    grad_down = -jnp.einsum(
        "htf,thd->hfd", key_hidden, scaled_values, preferred_element_type=jnp.float32
    )

    hidden_units = fast.shape[2]
    owners = 2 * zs
    grads = [a.astype(jnp.bfloat16) for a in (grad_gate, grad_up, grad_down)]
    whole = jnp.concatenate([grads[0], grads[1], grads[2][: owners - 2 * half]], axis=0)
    ninth = grads[2][owners - 2 * half :].reshape(owners, hidden_units // owners, head_dim)
    spread = jnp.concatenate([whole, ninth], axis=1)
    kept = jnp.where(is_first, spread[:zs], spread[zs:])
    got = swap_axis(jnp.where(is_first, spread[zs:], spread[:zs]), "c")
    summed = (kept.astype(jnp.float32) + got.astype(jnp.float32)).astype(jnp.bfloat16)
    parts = lax.all_to_all(summed, "zl", 0, 0, tiled=True)
    owned = jnp.sum(parts.astype(jnp.float32), axis=0)
    own, own_rows = owned[:hidden_units], owned[hidden_units:]
    small = own_rows.astype(jnp.bfloat16)
    small = jnp.concatenate([small, swap_axis(small, "c")], axis=0)
    small = lax.all_to_all(jnp.broadcast_to(small[None], (zs,) + small.shape), "zl", 0, 0, tiled=True)
    small = small.reshape(hidden_units, head_dim).astype(jnp.float32)

    shard_rows = previous.shape[2]
    current = orthogonalize(own, own).reshape(owners, 2, shard_rows, head_dim)
    outgoing = current.transpose(1, 0, 2, 3).reshape(2 * owners, shard_rows, head_dim)
    arrived = lax.all_to_all(outgoing, ("xh", "c", "zl"), 0, 0, tiled=True)
    arrived = arrived.reshape(2, owners, shard_rows, head_dim)
    last = orthogonalize(small, own_rows).reshape(2, shard_rows, head_dim)
    kept = jnp.where(is_low, last[0], last[1])
    got = swap_axis(jnp.where(is_low, last[1], last[0]), "xh")
    last = jnp.stack([jnp.where(is_low, kept, got), jnp.where(is_low, got, kept)])
    current = exchange(jnp.concatenate([arrived, last[:, None]], axis=1), 0).astype(jnp.float32)
    current = current.reshape(2, 3, half, shard_rows, head_dim).transpose(1, 0, 2, 3, 4)
    current = current.reshape(previous.shape)
    stepped = previous - update_scale * current
    rescale = jnp.sqrt(jnp.mean(previous * previous, axis=-1, keepdims=True) + 1e-06) * lax.rsqrt(
        jnp.mean(stepped * stepped, axis=-1, keepdims=True) + 1e-06
    )
    new_state = (stepped * rescale)[None, None]

    query = dots(my_columns, my_q) + dots(its_columns, swap_axis(my_q, "c"))
    query_rows = unit_rows(swish(by_head(query))).astype(jnp.bfloat16)
    gate_query = jnp.einsum(
        "thd,hfd->htf", query_rows, gate_fast, preferred_element_type=jnp.float32
    )
    up_query = jnp.einsum("thd,hfd->htf", query_rows, up_fast, preferred_element_type=jnp.float32)
    hidden = (swish(gate_query) * up_query).astype(jnp.bfloat16)
    mixture = jnp.einsum("htf,hfd->thd", hidden, down_fast, preferred_element_type=jnp.float32)
    head_out = (
        mixture * lax.rsqrt(jnp.mean(mixture * mixture, axis=-1, keepdims=True) + 1e-05)
    ).astype(jnp.bfloat16)
    ordered = head_out.reshape(2 * count, 2, zs, -1, rows).transpose(1, 0, 3, 2, 4)
    ordered = ordered.reshape(2, 2 * count, width // 2)
    branch_out = dots(jnp.where(is_first, ordered[0], ordered[1]), my_out) + dots(
        jnp.where(is_first, ordered[1], ordered[0]), swap_axis(my_out, "c")
    )
    from_pair = swap_axis(branch_out[count:].astype(jnp.bfloat16), "xh")
    passed = (
        mine.astype(jnp.float32) + (branch_out[:count] + from_pair.astype(jnp.float32))
    ).astype(jnp.bfloat16)
    passed = exchange(passed, 0)
    return (passed[None, None], new_state)


def solution(mesh):
    shape = (2, 2, 4, mesh.shape["sec"] // 2, 2, mesh.shape["dp"])
    split = Mesh(mesh.devices.reshape(shape), ("xh", "xl", "zl", "y", "c", "dp"))
    in_specs = (
        P("dp", CTX, None),
        P(SEC, "dp", CTX, None),
        P(SEC, CTX_DP, None),
        P(SEC, CTX_DP, None),
        P(SEC, CTX_DP, None),
        P(SEC, "dp", None, None, CTX, None),
    )
    out_specs = (P(SEC, "dp", CTX, None), P(SEC, "dp", None, None, CTX, None))
    return jax.shard_map(local, mesh=split, in_specs=in_specs, out_specs=out_specs, check_vma=False)
```

```python
import jax
import jax.numpy as jnp
from jax import lax
from jax.experimental import pallas as pl
from jax.sharding import Mesh
from jax.sharding import PartitionSpec as P


CTX = ("xh", "xl", "zl")
CTX_DP = CTX + ("dp",)
SEC = ("y", "c")
LANES = 128

linear_coef = 3.4445
cubic_coef = -4.775
quintic_coef = 2.0315
update_scale = 8.0
highest = lax.Precision.HIGHEST


def swish(values):
    return values * jax.nn.sigmoid(values)


def unit_rows(values):
    return values / jnp.sqrt(jnp.sum(values * values, axis=-1, keepdims=True) + 1e-06)


def swap_axis(block, axis):
    return lax.ppermute(block, axis, [(0, 1), (1, 0)])


def exchange(block, across):
    route = [
        (4 * x + 2 * a + b, 4 * (x ^ across) + 2 * b + a)
        for x in (0, 1)
        for a in (0, 1)
        for b in (0, 1)
    ]
    return lax.ppermute(block, ("xh", "xl", "c"), route)


def from_section_behind(block, across):
    ys = lax.axis_size("y")
    at = lambda x, a, y, b: ((2 * x + a) * ys + y) * 2 + b
    route = []
    for x in (0, 1):
        for layer in (0, 1):
            for y in range(ys):
                for k in (0, 1):
                    behind = (2 * y + layer - 1) % (2 * ys)
                    source = at(x ^ across, k, behind // 2, behind % 2)
                    route.append((source, at(x, layer, y, k)))
    return lax.ppermute(block, ("xh", "xl", "y", "c"), route)


def pair_shard(low, high, is_low, dim):
    kept = exchange(jnp.where(is_low, low, high), 0)
    got = exchange(jnp.where(is_low, high, low), 1)
    return jnp.concatenate([jnp.where(is_low, kept, got), jnp.where(is_low, got, kept)], axis=dim)


def ring_gather(block):
    dps = lax.axis_size("dp")
    n = lax.axis_size("zl") * dps
    middle = block.shape[0] // 2
    ring = [(i % (n // dps)) * dps + i // (n // dps) for i in range(n)]
    shift = lambda a, by: lax.ppermute(
        a, ("zl", "dp"), [(ring[i], ring[(i + by) % n]) for i in range(n)]
    )
    up = lambda a: shift(a, 1)
    down = lambda a: shift(a, -1)
    below, above = [block], [block]
    for _ in range(n // 2 - 1):
        above.append(down(above[-1]))
        below.append(up(below[-1]))
    far = [down(above[-1][:middle]), up(below[-1][middle:])]
    return jnp.concatenate(above + far + below[:0:-1], axis=0)


def line_gather(block, dim):
    n = lax.axis_size("zl")
    up = lambda a: lax.ppermute(a, "zl", [(i, i + 1) for i in range(n - 1)])
    down = lambda a: lax.ppermute(a, "zl", [(i + 1, i) for i in range(n - 1)])
    below, above = [block], [block]
    for _ in range(n - 1):
        above.append(down(above[-1]))
        below.append(up(below[-1]))
    both = jnp.concatenate(below[:0:-1] + above, axis=dim)
    size = block.shape[dim]
    start = (n - 1 - lax.axis_index("zl")) * size
    return lax.dynamic_slice_in_dim(both, start, n * size, axis=dim)


def dots(a, b):
    return jnp.dot(a, b, preferred_element_type=jnp.float32)


def dots_t(a, b):
    return lax.dot_general(a, b, (((1,), (1,)), ((), ())), preferred_element_type=jnp.float32)


def t_dots(a, b):
    return lax.dot_general(a, b, (((0,), (0,)), ((), ())), preferred_element_type=jnp.float32)


def key_rows_kernel(mine, its, key_a, key_b, value_a, value_b, rate_a, rate_b, keys, values):
    head = pl.program_id(0)
    a, b = mine[...], its[...]
    keys[0] = unit_rows(swish(dots(a, key_a[...]) + dots(b, key_b[...]))).astype(jnp.bfloat16)
    value_rows = (dots(a, value_a[...]) + dots(b, value_b[...])).astype(jnp.bfloat16)
    pre = dots(a, rate_a[...]) + dots(b, rate_b[...])
    rates = jnp.maximum(pre, 0.0) + jnp.log1p(jnp.exp(-jnp.abs(pre)))
    lanes = lax.broadcasted_iota(jnp.int32, rates.shape, 1)
    rate = jnp.sum(jnp.where(lanes == head, rates, 0.0), axis=1, keepdims=True)
    values[0] = (rate * value_rows.astype(jnp.float32)).astype(jnp.bfloat16)


def key_rows_of(mine, its, w_a, w_b, half, head_dim):
    tokens, depth = mine.shape
    whole = pl.BlockSpec((tokens, depth), lambda h: (0, 0))
    columns = lambda first: pl.BlockSpec((depth, head_dim), lambda h: (0, first + h))
    rates = pl.BlockSpec((depth, LANES), lambda h: (0, 2 * half * head_dim // LANES))
    out = pl.BlockSpec((1, tokens, head_dim), lambda h: (h, 0, 0))
    shape = jax.ShapeDtypeStruct((half, tokens, head_dim), jnp.bfloat16)
    return pl.pallas_call(
        key_rows_kernel,
        grid=(half,),
        in_specs=[whole, whole, columns(0), columns(0), columns(half), columns(half), rates, rates],
        out_specs=[out, out],
        out_shape=[shape, shape],
        name="key_rows",
    )(mine, its, w_a, w_b, w_a, w_b, w_a, w_b)


def gradient_kernel(keys, values, gate, up, down, grads):
    key, value = keys[0], values[0]
    gate_pre = dots_t(key, gate[0, 0])
    up_pre = dots_t(key, up[0, 0])
    sigma = jax.nn.sigmoid(gate_pre)
    gate_act = gate_pre * sigma
    key_hidden = (gate_act * up_pre).astype(jnp.bfloat16)
    hidden_grad = -dots_t(value, down[0, 0])
    up_grad = (hidden_grad * gate_act).astype(jnp.bfloat16)
    gate_grad = (hidden_grad * up_pre * sigma * (1.0 + gate_pre * (1.0 - sigma))).astype(
        jnp.bfloat16
    )
    grads[0, 0] = t_dots(gate_grad, key).astype(jnp.bfloat16)
    grads[1, 0] = t_dots(up_grad, key).astype(jnp.bfloat16)
    grads[2, 0] = (-t_dots(key_hidden, value)).astype(jnp.bfloat16)


def gradient_of(keys, values, fast):
    half, tokens, head_dim = keys.shape
    units = fast.shape[2]
    rows = pl.BlockSpec((1, tokens, head_dim), lambda h: (h, 0, 0))
    kind = lambda i: pl.BlockSpec((1, 1, units, head_dim), lambda h: (i, h, 0, 0))
    return pl.pallas_call(
        gradient_kernel,
        grid=(half,),
        in_specs=[rows, rows, kind(0), kind(1), kind(2)],
        out_specs=pl.BlockSpec((3, 1, units, head_dim), lambda h: (0, h, 0, 0)),
        out_shape=jax.ShapeDtypeStruct(fast.shape, jnp.bfloat16),
        name="gradient",
    )(keys, values, fast, fast, fast)


def query_kernel(mine, its, w_a, w_b, fast_a, fast_b, head_out):
    query = unit_rows(swish(dots(mine[...], w_a[...]) + dots(its[...], w_b[...])))
    query = query.astype(jnp.bfloat16)
    mixture = jnp.zeros(query.shape, jnp.float32)
    for fast in (fast_a, fast_b):
        hidden = swish(dots_t(query, fast[0, 0])) * dots_t(query, fast[1, 0])
        mixture = mixture + dots(hidden.astype(jnp.bfloat16), fast[2, 0])
    norm = lax.rsqrt(jnp.mean(mixture * mixture, axis=-1, keepdims=True) + 1e-05)
    head_out[...] = (mixture * norm).astype(jnp.bfloat16)


def head_out_of(mine, its, w_a, w_b, fast_a, fast_b):
    tokens, depth = mine.shape
    half, units, head_dim = fast_a.shape[1:]
    whole = pl.BlockSpec((tokens, depth), lambda h: (0, 0))
    columns = pl.BlockSpec((depth, head_dim), lambda h: (0, h))
    kinds = pl.BlockSpec((3, 1, units, head_dim), lambda h: (0, h, 0, 0))
    return pl.pallas_call(
        query_kernel,
        grid=(half,),
        in_specs=[whole, whole, columns, columns, kinds, kinds],
        out_specs=pl.BlockSpec((tokens, head_dim), lambda h: (0, h)),
        out_shape=jax.ShapeDtypeStruct((tokens, half * head_dim), jnp.bfloat16),
        name="head_out",
    )(mine, its, w_a, w_b, fast_a, fast_b)


def orthogonalize_kernel(gradient, rows, out):
    exact = lambda a, b: jnp.dot(a, b, precision=highest, preferred_element_type=jnp.float32)
    g = gradient[...]
    square = lax.dot_general(
        g, g, (((0,), (0,)), ((), ())), precision=highest, preferred_element_type=jnp.float32
    )
    size = square.shape[0]
    eye = lax.broadcasted_iota(jnp.int32, (size, size), 0) == lax.broadcasted_iota(
        jnp.int32, (size, size), 1
    )
    trace = jnp.sum(
        jnp.sum(jnp.where(eye, square, 0.0), axis=1, keepdims=True), axis=0, keepdims=True
    )
    inverse_norm = lax.rsqrt(trace + 1e-06)

    def polynomial(square):
        higher = cubic_coef * square + quintic_coef * exact(square, square)
        return jnp.where(eye, linear_coef, 0.0) + higher

    square = square * inverse_norm * inverse_norm
    first = polynomial(square)
    square = exact(first, exact(square, first))
    both = exact(first, polynomial(square))
    out[...] = exact(rows[...] * inverse_norm, both).astype(jnp.bfloat16)


def orthogonalize(gradient, rows):
    return pl.pallas_call(
        orthogonalize_kernel,
        out_shape=jax.ShapeDtypeStruct(rows.shape, jnp.bfloat16),
        name="orthogonalize",
    )(gradient, rows)


def layer(fresh_input, carried, qkv_weight, out_weight, rate_weight, fast_state):
    is_low = lax.axis_index("xh") == 0
    is_first = lax.axis_index("c") == 0
    heads = rate_weight.shape[2]
    head_dim = fast_state.shape[5]
    half = heads // 2
    width = half * head_dim
    rows = qkv_weight.shape[1]
    count, channels = fresh_input.shape[1:]
    by_core = lambda a, b: (jnp.where(is_first, a, b), jnp.where(is_first, b, a))

    w = qkv_weight[0]
    part = lambda i, h: w[:, (2 * i + h) * width : (2 * i + h + 1) * width]
    rate = lambda h: jnp.pad(
        rate_weight[0][:, h * half : (h + 1) * half], ((0, 0), (0, LANES - half))
    )
    low, high = (jnp.concatenate([part(1, h), part(2, h), rate(h)], axis=1) for h in (0, 1))
    shard_kv = pair_shard(low, high, is_low, 0)
    previous = fast_state[0, 0]
    shard = previous.astype(jnp.bfloat16)
    shard_fast = pair_shard(shard[:, :half], shard[:, half:], is_low, 2)

    is_last = lax.axis_index(SEC) == lax.axis_size(SEC) - 1
    source = jnp.where(is_last, fresh_input[0], carried[0, 0])
    mine = from_section_behind(source, 0)
    other = from_section_behind(source, 1)

    shard_q = pair_shard(part(0, 0), part(0, 1), is_low, 0)
    out_w = exchange(out_weight[0], 0)
    out_w = jnp.concatenate([out_w[:, : channels // 2], out_w[:, channels // 2 :]], axis=0)
    shard_qo = jnp.concatenate([shard_q, out_w], axis=1)

    my_kv = ring_gather(shard_kv)
    my_fast = line_gather(shard_fast, 2)
    my_qo = ring_gather(shard_qo)
    its_kv = swap_axis(my_kv, "c")
    its_fast = swap_axis(my_fast, "c")
    its_qo = swap_axis(my_qo, "c")

    zs = lax.axis_size("zl")
    ring_size = lax.axis_size(("dp", "zl"))
    at = lax.axis_index(("dp", "zl"))
    inputs = jnp.concatenate([mine, other], axis=0)
    ordered = inputs.reshape(2 * count, 2, 2, zs, -1, rows).transpose(2, 4, 3, 0, 1, 5)
    ordered = ordered.reshape(2, ring_size, 2 * count, 2 * rows)
    ordered = lax.dynamic_slice_in_dim(
        jnp.concatenate([ordered, ordered], axis=1), at, ring_size, axis=1
    )
    ordered = ordered.transpose(0, 2, 1, 3).reshape(2, 2 * count, channels // 2)
    my_columns, its_columns = by_core(ordered[0], ordered[1])

    keys, values = key_rows_of(my_columns, its_columns, my_kv, its_kv, half, head_dim)
    grads = by_core(gradient_of(keys, values, my_fast), gradient_of(keys, values, its_fast))
    hidden_units = 2 * my_fast.shape[2]
    grads = jnp.concatenate(grads, axis=2).reshape(3 * half, hidden_units, head_dim)

    owners = 2 * zs
    ninth = grads[owners].reshape(owners, hidden_units // owners, head_dim)
    spread = jnp.concatenate([grads[:owners], ninth], axis=1)
    kept, sent = by_core(spread[:zs], spread[zs:])
    got = swap_axis(sent, "c")
    summed = (kept.astype(jnp.float32) + got.astype(jnp.float32)).astype(jnp.bfloat16)
    parts = lax.all_to_all(summed, "zl", 0, 0, tiled=True)
    owned = jnp.sum(parts.astype(jnp.float32), axis=0)
    own, own_rows = owned[:hidden_units], owned[hidden_units:]
    small = own_rows.astype(jnp.bfloat16)
    small = jnp.concatenate([small, swap_axis(small, "c")], axis=0)
    small = lax.all_to_all(jnp.broadcast_to(small[None], (zs,) + small.shape), "zl", 0, 0, tiled=True)
    small = small.reshape(hidden_units, head_dim).astype(jnp.float32)

    shard_rows = previous.shape[2]
    current = orthogonalize(own, own).reshape(owners, 2, shard_rows, head_dim)
    outgoing = current.transpose(1, 0, 2, 3).reshape(2 * owners, shard_rows, head_dim)
    arrived = lax.all_to_all(outgoing, ("xh", "c", "zl"), 0, 0, tiled=True)
    arrived = arrived.reshape(2, owners, shard_rows, head_dim)
    last = orthogonalize(small, own_rows).reshape(2, shard_rows, head_dim)
    kept = jnp.where(is_low, last[0], last[1])
    got = swap_axis(jnp.where(is_low, last[1], last[0]), "xh")
    last = jnp.stack([jnp.where(is_low, kept, got), jnp.where(is_low, got, kept)])
    current = exchange(jnp.concatenate([arrived, last[:, None]], axis=1), 0).astype(jnp.float32)
    current = current.reshape(2, 3, half, shard_rows, head_dim).transpose(1, 0, 2, 3, 4)
    current = current.reshape(previous.shape)
    stepped = previous - update_scale * current
    rescale = jnp.sqrt(jnp.mean(previous * previous, axis=-1, keepdims=True) + 1e-06) * lax.rsqrt(
        jnp.mean(stepped * stepped, axis=-1, keepdims=True) + 1e-06
    )
    new_state = (stepped * rescale)[None, None]

    head_out = head_out_of(my_columns, its_columns, my_qo, its_qo, my_fast, its_fast)
    out_rows = jnp.stack(by_core(my_qo[:, width:], its_qo[:, width:]))
    out_rows = out_rows.reshape(2, ring_size, 2, rows, width)
    out_rows = lax.dynamic_slice_in_dim(
        jnp.concatenate([out_rows, out_rows], axis=1), ring_size - at, ring_size, axis=1
    )
    out_rows = out_rows.reshape(2, -1, zs, 2, rows, width).transpose(3, 0, 2, 1, 4, 5)
    out_rows = out_rows.reshape(2, width, width)
    branch_out = jnp.concatenate([dots(head_out, out_rows[0]), dots(head_out, out_rows[1])], axis=1)
    from_pair = swap_axis(branch_out[count:].astype(jnp.bfloat16), "xh")
    passed = (
        mine.astype(jnp.float32) + (branch_out[:count] + from_pair.astype(jnp.float32))
    ).astype(jnp.bfloat16)
    passed = exchange(passed, 0)
    return (passed[None, None], new_state)


def solution(mesh):
    shape = (2, 2, 4, mesh.shape["sec"] // 2, 2, mesh.shape["dp"])
    split = Mesh(mesh.devices.reshape(shape), ("xh", "xl", "zl", "y", "c", "dp"))
    in_specs = (
        P("dp", CTX, None),
        P(SEC, "dp", CTX, None),
        P(SEC, CTX_DP, None),
        P(SEC, CTX_DP, None),
        P(SEC, CTX_DP, None),
        P(SEC, "dp", None, None, CTX, None),
    )
    out_specs = (P(SEC, "dp", CTX, None), P(SEC, "dp", None, None, CTX, None))
    return jax.shard_map(layer, mesh=split, in_specs=in_specs, out_specs=out_specs, check_vma=False)
```

```python
import jax
import jax.numpy as jnp
from jax import lax
from jax.experimental import pallas as pl
from jax.sharding import Mesh
from jax.sharding import PartitionSpec as P


CTX = ("xh", "xl", "zl")
CTX_DP = CTX + ("dp",)
SEC = ("y", "c")
LANES = 128

linear_coef = 3.4445
cubic_coef = -4.775
quintic_coef = 2.0315
update_scale = 8.0


def swish(values):
    return values * jax.nn.sigmoid(values)


def unit_rows(values):
    return values / jnp.sqrt(jnp.sum(values * values, axis=-1, keepdims=True) + 1e-06)


def swap_axis(block, axis):
    return lax.ppermute(block, axis, [(0, 1), (1, 0)])


def exchange(block, across):
    route = [
        (4 * x + 2 * a + b, 4 * (x ^ across) + 2 * b + a)
        for x in (0, 1)
        for a in (0, 1)
        for b in (0, 1)
    ]
    return lax.ppermute(block, ("xh", "xl", "c"), route)


def from_section_behind(block, across):
    ys = lax.axis_size("y")
    at = lambda x, a, y, b: ((2 * x + a) * ys + y) * 2 + b
    route = []
    for x in (0, 1):
        for layer in (0, 1):
            for y in range(ys):
                for k in (0, 1):
                    behind = (2 * y + layer - 1) % (2 * ys)
                    source = at(x ^ across, k, behind // 2, behind % 2)
                    route.append((source, at(x, layer, y, k)))
    return lax.ppermute(block, ("xh", "xl", "y", "c"), route)


def pair_shard(low, high, is_low, dim):
    kept = exchange(jnp.where(is_low, low, high), 0)
    got = exchange(jnp.where(is_low, high, low), 1)
    return jnp.concatenate([jnp.where(is_low, kept, got), jnp.where(is_low, got, kept)], axis=dim)


def ring_gather(block):
    dps = lax.axis_size("dp")
    n = lax.axis_size("zl") * dps
    middle = block.shape[0] // 2
    ring = [(i % (n // dps)) * dps + i // (n // dps) for i in range(n)]
    shift = lambda a, by: lax.ppermute(
        a, ("zl", "dp"), [(ring[i], ring[(i + by) % n]) for i in range(n)]
    )
    up = lambda a: shift(a, 1)
    down = lambda a: shift(a, -1)
    below, above = [block], [block]
    for _ in range(n // 2 - 1):
        above.append(down(above[-1]))
        below.append(up(below[-1]))
    far = [down(above[-1][:middle]), up(below[-1][middle:])]
    return jnp.concatenate(above + below[:0:-1] + far, axis=0)


def line_gather(block, dim):
    n = lax.axis_size("zl")
    up = lambda a: lax.ppermute(a, "zl", [(i, i + 1) for i in range(n - 1)])
    down = lambda a: lax.ppermute(a, "zl", [(i + 1, i) for i in range(n - 1)])
    below, above = [block], [block]
    for _ in range(n - 1):
        above.append(down(above[-1]))
        below.append(up(below[-1]))
    both = jnp.concatenate(below[:0:-1] + above, axis=dim)
    size = block.shape[dim]
    start = (n - 1 - lax.axis_index("zl")) * size
    return lax.dynamic_slice_in_dim(both, start, n * size, axis=dim)


def dots(a, b):
    return jnp.dot(a, b, preferred_element_type=jnp.float32)


def dots_t(a, b):
    return lax.dot_general(a, b, (((1,), (1,)), ((), ())), preferred_element_type=jnp.float32)


def t_dots(a, b):
    return lax.dot_general(a, b, (((0,), (0,)), ((), ())), preferred_element_type=jnp.float32)


def key_rows_kernel(mine, its, key_a, key_b, value_a, value_b, rate_a, rate_b, keys, values):
    head = pl.program_id(0)
    a, b = mine[...], its[...]
    keys[0] = unit_rows(swish(dots(a, key_a[...]) + dots(b, key_b[...]))).astype(jnp.bfloat16)
    value_rows = (dots(a, value_a[...]) + dots(b, value_b[...])).astype(jnp.bfloat16)
    pre = dots(a, rate_a[...]) + dots(b, rate_b[...])
    rates = jnp.maximum(pre, 0.0) + jnp.log1p(jnp.exp(-jnp.abs(pre)))
    lanes = lax.broadcasted_iota(jnp.int32, rates.shape, 1)
    rate = jnp.sum(jnp.where(lanes == head, rates, 0.0), axis=1, keepdims=True)
    values[0] = (rate * value_rows.astype(jnp.float32)).astype(jnp.bfloat16)


def key_rows_of(mine, its, w_a, w_b, half, head_dim):
    tokens, depth = mine.shape
    whole = pl.BlockSpec((tokens, depth), lambda h: (0, 0))
    columns = lambda first: pl.BlockSpec((depth, head_dim), lambda h: (0, first + h))
    rates = pl.BlockSpec((depth, LANES), lambda h: (0, 2 * half * head_dim // LANES))
    out = pl.BlockSpec((1, tokens, head_dim), lambda h: (h, 0, 0))
    shape = jax.ShapeDtypeStruct((half, tokens, head_dim), jnp.bfloat16)
    return pl.pallas_call(
        key_rows_kernel,
        grid=(half,),
        in_specs=[whole, whole, columns(0), columns(0), columns(half), columns(half), rates, rates],
        out_specs=[out, out],
        out_shape=[shape, shape],
        name="key_rows",
    )(mine, its, w_a, w_b, w_a, w_b, w_a, w_b)


def gradient_kernel(keys, values, gate, up, down, grads):
    key, value = keys[0], values[0]
    gate_pre = dots_t(key, gate[0, 0])
    up_pre = dots_t(key, up[0, 0])
    sigma = jax.nn.sigmoid(gate_pre)
    gate_act = gate_pre * sigma
    key_hidden = (gate_act * up_pre).astype(jnp.bfloat16)
    hidden_grad = -dots_t(value, down[0, 0])
    up_grad = (hidden_grad * gate_act).astype(jnp.bfloat16)
    gate_grad = (hidden_grad * up_pre * sigma * (1.0 + gate_pre * (1.0 - sigma))).astype(
        jnp.bfloat16
    )
    grads[0, 0] = t_dots(gate_grad, key).astype(jnp.bfloat16)
    grads[1, 0] = t_dots(up_grad, key).astype(jnp.bfloat16)
    grads[2, 0] = (-t_dots(key_hidden, value)).astype(jnp.bfloat16)


def gradient_of(keys, values, fast):
    half, tokens, head_dim = keys.shape
    units = fast.shape[2]
    rows = pl.BlockSpec((1, tokens, head_dim), lambda h: (h, 0, 0))
    kind = lambda i: pl.BlockSpec((1, 1, units, head_dim), lambda h: (i, h, 0, 0))
    return pl.pallas_call(
        gradient_kernel,
        grid=(half,),
        in_specs=[rows, rows, kind(0), kind(1), kind(2)],
        out_specs=pl.BlockSpec((3, 1, units, head_dim), lambda h: (0, h, 0, 0)),
        out_shape=jax.ShapeDtypeStruct(fast.shape, jnp.bfloat16),
        name="gradient",
    )(keys, values, fast, fast, fast)


def query_kernel(mine, its, w_a, w_b, fast_a, fast_b, head_out):
    query = unit_rows(swish(dots(mine[...], w_a[...]) + dots(its[...], w_b[...])))
    query = query.astype(jnp.bfloat16)
    mixture = jnp.zeros(query.shape, jnp.float32)
    for fast in (fast_a, fast_b):
        hidden = swish(dots_t(query, fast[0, 0])) * dots_t(query, fast[1, 0])
        mixture = mixture + dots(hidden.astype(jnp.bfloat16), fast[2, 0])
    norm = lax.rsqrt(jnp.mean(mixture * mixture, axis=-1, keepdims=True) + 1e-05)
    head_out[...] = (mixture * norm).astype(jnp.bfloat16)


def head_out_of(mine, its, w_a, w_b, fast_a, fast_b):
    tokens, depth = mine.shape
    half, units, head_dim = fast_a.shape[1:]
    whole = pl.BlockSpec((tokens, depth), lambda h: (0, 0))
    columns = pl.BlockSpec((depth, head_dim), lambda h: (0, h))
    kinds = pl.BlockSpec((3, 1, units, head_dim), lambda h: (0, h, 0, 0))
    return pl.pallas_call(
        query_kernel,
        grid=(half,),
        in_specs=[whole, whole, columns, columns, kinds, kinds],
        out_specs=pl.BlockSpec((tokens, head_dim), lambda h: (0, h)),
        out_shape=jax.ShapeDtypeStruct((tokens, half * head_dim), jnp.bfloat16),
        name="head_out",
    )(mine, its, w_a, w_b, fast_a, fast_b)


def orthogonalize_kernel(gradient, rows, out):
    def halves(a):
        top = a.astype(jnp.bfloat16)
        return top, (a - top.astype(jnp.float32)).astype(jnp.bfloat16)

    def exact(a, b, product=dots):
        (a_top, a_rest), (b_top, b_rest) = halves(a), halves(b)
        return product(a_top, b_top) + (product(a_top, b_rest) + product(a_rest, b_top))

    g = gradient[...]
    square = exact(g, g, t_dots)
    size = square.shape[0]
    eye = lax.broadcasted_iota(jnp.int32, (size, size), 0) == lax.broadcasted_iota(
        jnp.int32, (size, size), 1
    )
    trace = jnp.sum(
        jnp.sum(jnp.where(eye, square, 0.0), axis=1, keepdims=True), axis=0, keepdims=True
    )
    inverse_norm = lax.rsqrt(trace + 1e-06)

    def polynomial(square):
        higher = cubic_coef * square + quintic_coef * exact(square, square)
        return jnp.where(eye, linear_coef, 0.0) + higher

    square = square * inverse_norm * inverse_norm
    first = polynomial(square)
    square = exact(first, exact(square, first))
    both = exact(first, polynomial(square))
    out[...] = exact(rows[...] * inverse_norm, both).astype(jnp.bfloat16)


def orthogonalize(gradient, rows):
    return pl.pallas_call(
        orthogonalize_kernel,
        out_shape=jax.ShapeDtypeStruct(rows.shape, jnp.bfloat16),
        name="orthogonalize",
    )(gradient, rows)


def columns_of(mine, other, rows, at, far, is_first):
    tokens = mine.shape[0] + other.shape[0]
    zs = lax.axis_size("zl")
    inputs = jnp.concatenate([mine, other], axis=0)
    ordered = inputs.reshape(tokens, 2, 2, zs, -1, rows).transpose(2, 4, 3, 0, 1, 5)
    ordered = ordered.reshape(2, 2 * far, tokens, 2 * rows)
    ordered = jnp.concatenate([ordered, ordered], axis=1)
    ordered = lax.dynamic_slice_in_dim(ordered, at, 2 * far, axis=1)
    ordered = jnp.concatenate(
        [ordered[:, :far], ordered[:, far + 1 :], ordered[:, far : far + 1]], axis=1
    )
    ordered = ordered.transpose(0, 2, 1, 3).reshape(2, tokens, -1)
    return (
        jnp.where(is_first, ordered[0], ordered[1]),
        jnp.where(is_first, ordered[1], ordered[0]),
    )


def layer(fresh_input, carried, qkv_weight, out_weight, rate_weight, fast_state):
    is_low = lax.axis_index("xh") == 0
    is_first = lax.axis_index("c") == 0
    heads = rate_weight.shape[2]
    head_dim = fast_state.shape[5]
    half = heads // 2
    width = half * head_dim
    rows = qkv_weight.shape[1]
    count, channels = fresh_input.shape[1:]
    by_core = lambda a, b: (jnp.where(is_first, a, b), jnp.where(is_first, b, a))

    w = qkv_weight[0]
    part = lambda i, h: w[:, (2 * i + h) * width : (2 * i + h + 1) * width]
    rate = lambda h: jnp.pad(
        rate_weight[0][:, h * half : (h + 1) * half], ((0, 0), (0, LANES - half))
    )
    low, high = (jnp.concatenate([part(1, h), part(2, h), rate(h)], axis=1) for h in (0, 1))
    shard_kv = pair_shard(low, high, is_low, 0)
    previous = fast_state[0, 0]
    shard = previous.astype(jnp.bfloat16)
    shard_fast = pair_shard(shard[:, :half], shard[:, half:], is_low, 2)

    is_last = lax.axis_index(SEC) == lax.axis_size(SEC) - 1
    source = jnp.where(is_last, fresh_input[0], carried[0, 0])
    mine = from_section_behind(source, 0)
    other = from_section_behind(source, 1)

    shard_q = pair_shard(part(0, 0), part(0, 1), is_low, 0)
    out_w = exchange(out_weight[0], 0)
    out_w = jnp.concatenate([out_w[:, : channels // 2], out_w[:, channels // 2 :]], axis=0)
    shard_qo = jnp.concatenate([shard_q, out_w], axis=1)

    my_kv = ring_gather(shard_kv)
    my_fast = line_gather(shard_fast, 2)
    my_qo = ring_gather(shard_qo)
    its_kv = swap_axis(my_kv, "c")
    its_fast = swap_axis(my_fast, "c")
    its_qo = swap_axis(my_qo, "c")

    zs = lax.axis_size("zl")
    ring_size = lax.axis_size(("dp", "zl"))
    at = lax.axis_index(("dp", "zl"))
    far = ring_size // 2
    my_columns, its_columns = columns_of(mine, other, rows, at, far, is_first)

    keys, values = key_rows_of(my_columns, its_columns, my_kv, its_kv, half, head_dim)
    grads = gradient_of(keys, values, my_fast)
    grads = by_core(grads, gradient_of(keys, values, its_fast))
    hidden_units = 2 * my_fast.shape[2]
    grads = jnp.concatenate(grads, axis=2).reshape(3 * half, hidden_units, head_dim)

    owners = 2 * zs
    ninth = grads[owners].reshape(owners, hidden_units // owners, head_dim)
    spread = jnp.concatenate([grads[:owners], ninth], axis=1)
    kept, sent = by_core(spread[:zs], spread[zs:])
    got = swap_axis(sent, "c")
    summed = (kept.astype(jnp.float32) + got.astype(jnp.float32)).astype(jnp.bfloat16)
    parts = lax.all_to_all(summed, "zl", 0, 0, tiled=True)
    owned = jnp.sum(parts.astype(jnp.float32), axis=0)
    own, own_rows = owned[:hidden_units], owned[hidden_units:]
    small = own_rows.astype(jnp.bfloat16)
    small = jnp.concatenate([small, swap_axis(small, "c")], axis=0)
    small = lax.all_to_all(jnp.broadcast_to(small[None], (zs,) + small.shape), "zl", 0, 0, tiled=True)
    small = small.reshape(hidden_units, head_dim).astype(jnp.float32)

    shard_rows = previous.shape[2]
    current = orthogonalize(own, own).reshape(owners, 2, shard_rows, head_dim)
    outgoing = current.transpose(1, 0, 2, 3).reshape(2 * owners, shard_rows, head_dim)
    arrived = lax.all_to_all(outgoing, ("xh", "c", "zl"), 0, 0, tiled=True)
    arrived = arrived.reshape(2, owners, shard_rows, head_dim)
    last = orthogonalize(small, own_rows).reshape(2, shard_rows, head_dim)
    last = pair_shard(last[:1], last[1:], is_low, 0)[:, None]
    current = jnp.concatenate([exchange(arrived, 0), last], axis=1).astype(jnp.float32)
    current = current.reshape(2, 3, half, shard_rows, head_dim).transpose(1, 0, 2, 3, 4)
    current = current.reshape(previous.shape)
    stepped = previous - update_scale * current
    rescale = jnp.sqrt(jnp.mean(previous * previous, axis=-1, keepdims=True) + 1e-06) * lax.rsqrt(
        jnp.mean(stepped * stepped, axis=-1, keepdims=True) + 1e-06
    )
    new_state = (stepped * rescale)[None, None]

    head_out = head_out_of(my_columns, its_columns, my_qo, its_qo, my_fast, its_fast)
    out_rows = jnp.stack(by_core(my_qo[:, width:], its_qo[:, width:]))
    out_rows = out_rows.reshape(2, ring_size, 2, rows, width)
    out_rows = jnp.concatenate([out_rows[:, :far], out_rows[:, -1:], out_rows[:, far:-1]], axis=1)
    out_rows = lax.dynamic_slice_in_dim(
        jnp.concatenate([out_rows, out_rows], axis=1), ring_size - at, ring_size, axis=1
    )
    out_rows = out_rows.reshape(2, -1, zs, 2, rows, width).transpose(3, 0, 2, 1, 4, 5)
    out_rows = out_rows.reshape(2, width, width)
    branch_out = jnp.concatenate([dots(head_out, a) for a in out_rows], axis=1)
    from_pair = swap_axis(branch_out[count:].astype(jnp.bfloat16), "xh")
    passed = (
        mine.astype(jnp.float32) + (branch_out[:count] + from_pair.astype(jnp.float32))
    ).astype(jnp.bfloat16)
    passed = exchange(passed, 0)
    return (passed[None, None], new_state)


def solution(mesh):
    shape = (2, 2, 4, mesh.shape["sec"] // 2, 2, mesh.shape["dp"])
    split = Mesh(mesh.devices.reshape(shape), ("xh", "xl", "zl", "y", "c", "dp"))
    in_specs = (
        P("dp", CTX, None),
        P(SEC, "dp", CTX, None),
        P(SEC, CTX_DP, None),
        P(SEC, CTX_DP, None),
        P(SEC, CTX_DP, None),
        P(SEC, "dp", None, None, CTX, None),
    )
    out_specs = (P(SEC, "dp", CTX, None), P(SEC, "dp", None, None, CTX, None))
    return jax.shard_map(layer, mesh=split, in_specs=in_specs, out_specs=out_specs, check_vma=False)
```
